256 devices in a mesh: blk: 128 (over x_hi, z, y, core), grp: 2 (over x_lo).
Axes of the slice: x: 4 (x_hi: 2, x_lo: 2; x = x_hi * 2 + x_lo), y: 4, z: 8, core: 2. Of those that a mesh axis runs over, the one named last changes fastest.
Arguments:
- layer_one: bfloat16 [14336, 1024], P(('blk', 'grp')), may hold values from -6 to 6
- layer_two: bfloat16 [14336, 1024], P(('blk', 'grp')), may hold values from -6 to 6
- spread: int32 [2], replicated, may hold values from 1024 to 4096
Outputs:
- profiles: float32 [2, 14336], P(None, ('blk', 'grp'))
- alignment: float32 [], replicated
The draws below stay inside these ranges and needn't reach their ends.
All inputs are finite; a program needn't handle non-finite values.
Results may differ from the reference program's by a relative error of at most 0.0003.
Values may be sent and summed in bfloat16 or wider, within the bound.
No kernel may reach another device: no remote copies, remote signals or barrier semaphores. Data moves between devices by JAX's collectives and lax.ppermute only.
A program may use at most 128 MiB of HBM per device.

```python
import jax
import jax.numpy as jnp
from jax import lax

D = 1024
ROWS_DEV = 56
N = 14336


def steps_of(own_key, extent, pieces, least, high):
    def one(axis_at, parts):
        steps = jax.random.uniform(jax.random.fold_in(jax.random.fold_in(own_key, 6), axis_at), (parts,), jnp.float32, least / len(pieces), high / len(pieces))
        return jnp.repeat(jnp.exp(steps), extent[axis_at] // parts).reshape((-1,) + (1,) * (len(extent) - axis_at - 1))

    level = one(*pieces[0])
    for cut in pieces[1:]:
        level = level * one(*cut)
    return level


def normal_values(own_key, dims, scale, bound, shards=(), kind=jnp.bfloat16):
    result = scale * jax.random.normal(own_key, dims, jnp.float32)
    if shards:
        result = result * steps_of(own_key, dims, shards, -0.22, 0.18)
    return jnp.clip(result, -bound, bound).astype(kind)


def setup_inputs(seed: int = 0) -> dict:
    streams_of = jax.random.split(jax.random.key(seed), 4)
    return {
        "layer_one": normal_values(streams_of[0], (N, D), 1.0, 6.0, ((0, 256),)),
        "layer_two": normal_values(streams_of[1], (N, D), 1.0, 6.0, ((0, 256),)),
        "spread": jax.random.randint(streams_of[2], (2,), D, 4 * D + 1).astype(jnp.int32),
    }


def reference(layer_one, layer_two, spread):
    total = layer_one.shape[0]
    block_rows = 2 * ROWS_DEV
    scales = spread.astype(jnp.float32)
    offsets = jnp.exp(-D / scales)
    sq_one = lax.optimization_barrier(jnp.sum(layer_one.astype(jnp.float32) ** 2, axis=1))
    sq_two = lax.optimization_barrier(jnp.sum(layer_two.astype(jnp.float32) ** 2, axis=1))

    def kernel(rows, sq_rows, whole, sq_whole, scale, offset):
        inner = lax.dot_general(rows, whole, (((1,), (1,)), ((), ())), preferred_element_type=jnp.float32)
        dist = sq_rows[:, None] + sq_whole[None, :] - 2.0 * inner
        return jnp.exp(-dist / (2.0 * scale)) - offset

    def one_block(index):
        start = index * block_rows
        rows_one = lax.dynamic_slice_in_dim(layer_one, start, block_rows, 0)
        rows_two = lax.dynamic_slice_in_dim(layer_two, start, block_rows, 0)
        norm_one = lax.dynamic_slice_in_dim(sq_one, start, block_rows, 0)
        norm_two = lax.dynamic_slice_in_dim(sq_two, start, block_rows, 0)
        first = kernel(rows_one, norm_one, layer_one, sq_one, scales[0], offsets[0])
        second = kernel(rows_two, norm_two, layer_two, sq_two, scales[1], offsets[1])
        return (lax.optimization_barrier(jnp.sum(first, axis=1)), lax.optimization_barrier(jnp.sum(second, axis=1)), jnp.sum(first * second), jnp.sum(first * first), jnp.sum(second * second))
    results = lax.map(one_block, jnp.arange(total // block_rows, dtype=jnp.int32))
    row_one = results[0].reshape(-1)
    row_two = results[1].reshape(-1)
    cross, self_one, self_two = (jnp.sum(results[2]), jnp.sum(results[3]), jnp.sum(results[4]))
    sum_one, sum_two = (jnp.sum(row_one), jnp.sum(row_two))
    c_cross = jnp.sum(row_one * row_two)
    c_one = jnp.sum(row_one * row_one)
    c_two = jnp.sum(row_two * row_two)
    h_cross = cross - 2.0 * c_cross / total + sum_one * sum_two / (total * total)
    h_one = self_one - 2.0 * c_one / total + sum_one * sum_one / (total * total)
    h_two = self_two - 2.0 * c_two / total + sum_two * sum_two / (total * total)
    alignment = h_cross / jnp.sqrt(h_one * h_two)
    profiles = jnp.stack([row_one / jnp.sqrt(c_one / total), row_two / jnp.sqrt(c_two / total)])
    return (profiles, alignment)
```

```python
import functools
import math

import jax
import jax.numpy as jnp
from jax import lax
from jax.experimental import pallas as pl
from jax.experimental.pallas import tpu as pltpu
from jax.sharding import Mesh
from jax.sharding import PartitionSpec as P

D = 1024
AXES = ("x_hi", "z", "y", "core", "x_lo")
LINE = ("z", "core")
NX, NY, NZ, NC = (4, 4, 8, 2)
LOG2E = math.log2(math.e)


def linear(x, y, z, core):
    return (((x // 2 * NZ + z) * NY + y) * NC + core) * 2 + x % 2


def move(array, where):
    pairs = []
    for x in range(NX):
        for y in range(NY):
            for z in range(NZ):
                for core in range(NC):
                    tx, ty, tz, tcore = where(x, y, z, core)
                    pairs.append((linear(x, y, z, core), linear(tx % NX, ty % NY, tz % NZ, tcore % NC)))
    return lax.ppermute(array, AXES, pairs)


def shift(array, first, second):
    def where(x, y, z, core):
        dx, dy = (first, second) if core == 0 else (second, first)
        return x + dx, y + dy, z, core

    return move(array, where)


def gram_body(spread_ref, z_ref, *refs):
    pieces, out_ref, scaled_ref = refs[:-2], refs[-2], refs[-1]
    width = z_ref.shape[1]
    scales = [spread_ref[0].astype(jnp.float32), spread_ref[1].astype(jnp.float32)]
    factors = []
    offsets = []
    for layer in range(2):
        scale = jnp.full((1, 128), scales[layer], jnp.float32)
        factors.append((LOG2E / scale)[:, :1])
        offsets.append(jnp.exp(-D / scale)[:, :1])
        for start in range(0, width, 128):
            rows = z_ref[layer, start : start + 128, :].astype(jnp.float32)
            square = rows * rows
            folded = square[:, :128]
            for lane in range(128, D, 128):
                folded = folded + square[:, lane : lane + 128]
            sums = jnp.sum(folded.T, axis=0, keepdims=True)
            scaled_ref[layer : layer + 1, start : start + 128] = sums * (0.5 * factors[layer])
    sums = [jnp.zeros((8, width), jnp.float32) for _ in range(5)]

    def fold(array):
        parts = array.reshape(array.shape[0] // 8, 8, width)
        return jnp.sum(parts, axis=0)

    for piece in pieces:
        tall = piece.shape[1]
        step = 112 if tall % 112 == 0 else tall
        for start in range(0, tall, step):
            kernels = []
            for layer in range(2):
                rows = piece[layer, start : start + step, :]
                inner = lax.dot_general(
                    rows, z_ref[layer], (((1,), (1,)), ((), ())), preferred_element_type=jnp.float32
                )
                wide = rows.astype(jnp.float32)
                norms = jnp.sum(wide * wide, axis=1, keepdims=True) * (0.5 * factors[layer])
                power = inner * factors[layer] - norms - scaled_ref[layer : layer + 1, :]
                kernels.append(jnp.exp2(power) - offsets[layer])
            one, two = kernels
            for at, term in enumerate((one, two, one * two, one * one, two * two)):
                sums[at] = sums[at] + fold(term)
    for at in range(5):
        out_ref[at : at + 1, :] = jnp.sum(sums[at], axis=0, keepdims=True)
    out_ref[5:8, :] = jnp.zeros((3, width), jnp.float32)


def gram(spread, line, pieces):
    width = line.shape[1]
    vmem = pl.BlockSpec(memory_space=pltpu.VMEM)
    rows = sum(piece.shape[1] for piece in pieces)
    return pl.pallas_call(
        gram_body,
        out_shape=jax.ShapeDtypeStruct((8, width), jnp.float32),
        in_specs=[pl.BlockSpec(memory_space=pltpu.SMEM), vmem] + [vmem] * len(pieces),
        out_specs=vmem,
        scratch_shapes=[pltpu.VMEM((2, width), jnp.float32)],
        compiler_params=pltpu.CompilerParams(vmem_limit_bytes=40 << 20),
        cost_estimate=pl.CostEstimate(
            flops=4 * rows * width * D, bytes_accessed=4 * (rows + width) * D, transcendentals=2 * rows * width
        ),
        name="gram",
    )(spread, line, *pieces)


def shards(layer_one, layer_two, spread):
    own = jnp.stack([layer_one, layer_two])
    count = own.shape[1]
    line = lax.all_gather(own, LINE, axis=1, tiled=True)
    near = [shift(own, 1, 0), shift(own, -1, 0), shift(own, 2, 0)]
    strip = jnp.concatenate([own] + near, axis=1)
    pieces = [strip, shift(strip, 0, 1), shift(strip, 0, -1), shift(strip, 0, 2)]
    part = gram(spread, line, pieces)
    part = part + move(part, lambda x, y, z, core: (x, y, z, core ^ 1))
    for bit in (1, 2, 4):
        part = part + move(part, lambda x, y, z, core: (x, y, z ^ bit, core))
    total = count * lax.axis_size(AXES)
    r_one, r_two = part[0], part[1]
    scalars = jnp.stack(
        [r_one, r_two, part[2], part[3], part[4], r_one * r_two, r_one * r_one, r_two * r_two]
    )
    scalars = jnp.sum(scalars.reshape(8, part.shape[1] // 128, 128), axis=1)
    scalars = scalars + move(scalars, lambda x, y, z, core: (x ^ 1, y, z, core))
    scalars = scalars + move(scalars, lambda x, y, z, core: (x ^ 2, y, z, core))
    scalars = lax.psum(scalars, "y")
    scalars = jnp.sum(scalars, axis=1)
    sum_one, sum_two, f_cross, f_one, f_two, c_cross, c_one, c_two = (scalars[at] for at in range(8))
    h_cross = f_cross - 2.0 * c_cross / total + sum_one * sum_two / (total * total)
    h_one = f_one - 2.0 * c_one / total + sum_one * sum_one / (total * total)
    h_two = f_two - 2.0 * c_two / total + sum_two * sum_two / (total * total)
    alignment = h_cross / jnp.sqrt(h_one * h_two)
    mine = lax.dynamic_slice(part, (0, lax.axis_index(LINE) * count), (2, count))
    profiles = mine / jnp.sqrt(jnp.stack([c_one, c_two]) / total)[:, None]
    return (profiles, alignment)


def solution(mesh):
    finer = Mesh(mesh.devices.reshape(2, NZ, NY, NC, 2), AXES)
    return jax.shard_map(
        shards,
        mesh=finer,
        in_specs=(P(AXES, None), P(AXES, None), P()),
        out_specs=(P(None, AXES), P()),
        check_vma=False,
    )
```

```python
import functools
import math

import jax
import jax.numpy as jnp
from jax import lax
from jax.experimental import pallas as pl
from jax.experimental.pallas import tpu as pltpu
from jax.sharding import Mesh
from jax.sharding import PartitionSpec as P

D = 1024
AXES = ("x_hi", "z", "y", "core", "x_lo")
LINE = ("z", "core")
NX, NY, NZ, NC = (4, 4, 8, 2)
LOG2E = math.log2(math.e)


def linear(x, y, z, core):
    return (((x // 2 * NZ + z) * NY + y) * NC + core) * 2 + x % 2


def move(array, where):
    pairs = []
    for x in range(NX):
        for y in range(NY):
            for z in range(NZ):
                for core in range(NC):
                    tx, ty, tz, tcore = where(x, y, z, core)
                    pairs.append((linear(x, y, z, core), linear(tx % NX, ty % NY, tz % NZ, tcore % NC)))
    return lax.ppermute(array, AXES, pairs)


def shift(array, first, second):
    def where(x, y, z, core):
        dx, dy = (first, second) if core == 0 else (second, first)
        return x + dx, y + dy, z, core

    return move(array, where)


def gram_body(spread_ref, z_ref, *refs):
    pieces, out_ref, scaled_ref = refs[:-2], refs[-2], refs[-1]
    width = z_ref.shape[1]
    scales = [spread_ref[0].astype(jnp.float32), spread_ref[1].astype(jnp.float32)]
    factors = []
    offsets = []
    for layer in range(2):
        scale = jnp.full((1, 128), scales[layer], jnp.float32)
        factors.append((LOG2E / scale)[:, :1])
        offsets.append(jnp.exp(-D / scale)[:, :1])
        for start in range(0, width, 128):
            rows = z_ref[layer, start : start + 128, :].astype(jnp.float32)
            square = rows * rows
            folded = square[:, :128]
            for lane in range(128, D, 128):
                folded = folded + square[:, lane : lane + 128]
            sums = jnp.sum(folded.T, axis=0, keepdims=True)
            scaled_ref[layer : layer + 1, start : start + 128] = sums * (0.5 * factors[layer])
    sums = [jnp.zeros((8, width), jnp.float32) for _ in range(5)]

    def fold(array):
        parts = array.reshape(array.shape[0] // 8, 8, width)
        return jnp.sum(parts, axis=0)

    for piece in pieces:
        tall = piece.shape[1]
        step = 112 if tall % 112 == 0 else tall
        for start in range(0, tall, step):
            kernels = []
            for layer in range(2):
                rows = piece[layer, start : start + step, :]
                inner = lax.dot_general(
                    rows, z_ref[layer], (((1,), (1,)), ((), ())), preferred_element_type=jnp.float32
                )
                wide = rows.astype(jnp.float32)
                norms = jnp.sum(wide * wide, axis=1, keepdims=True) * (0.5 * factors[layer])
                power = inner * factors[layer] - norms - scaled_ref[layer : layer + 1, :]
                kernels.append(jnp.exp2(power) - offsets[layer])
            one, two = kernels
            for at, term in enumerate((one, two, one * two, one * one, two * two)):
                sums[at] = sums[at] + fold(term)
    for at in range(5):
        out_ref[at : at + 1, :] = jnp.sum(sums[at], axis=0, keepdims=True)
    out_ref[5:8, :] = jnp.zeros((3, width), jnp.float32)


def gram(spread, line, pieces):
    width = line.shape[1]
    vmem = pl.BlockSpec(memory_space=pltpu.VMEM)
    rows = sum(piece.shape[1] for piece in pieces)
    return pl.pallas_call(
        gram_body,
        out_shape=jax.ShapeDtypeStruct((8, width), jnp.float32),
        in_specs=[pl.BlockSpec(memory_space=pltpu.SMEM), vmem] + [vmem] * len(pieces),
        out_specs=vmem,
        scratch_shapes=[pltpu.VMEM((2, width), jnp.float32)],
        compiler_params=pltpu.CompilerParams(vmem_limit_bytes=16 << 20),
        cost_estimate=pl.CostEstimate(
            flops=4 * rows * width * D, bytes_accessed=4 * (rows + width) * D, transcendentals=2 * rows * width
        ),
        name="gram",
    )(spread, line, *pieces)


def swap(array):
    return move(array, lambda x, y, z, core: (x, y, z, 1 - core))


def line_sum(array):
    array = array + swap(array)
    for bit in (1, 2, 4):
        array = array + move(array, lambda x, y, z, core: (x, y, z ^ bit, core))
    return array


def plane_sum(array):
    for stage in range(2):
        parts = [shift(array, *((step, 0) if stage == 0 else (0, step))) for step in (1, -1, 2)]
        array = (array + parts[2]) + (parts[0] + parts[1])
    return 0.5 * (array + swap(array))


def finish_body(total, count, part_ref, sums_ref, profiles_ref, alignment_ref):
    sums = jnp.sum(sums_ref[...], axis=1, keepdims=True)
    sum_one, sum_two, f_cross, f_one, f_two, c_cross, c_one, c_two = (sums[at : at + 1, :] for at in range(8))
    h_cross = f_cross - 2.0 * c_cross / total + sum_one * sum_two / (total * total)
    h_one = f_one - 2.0 * c_one / total + sum_one * sum_one / (total * total)
    h_two = f_two - 2.0 * c_two / total + sum_two * sum_two / (total * total)
    alignment_ref[...] = h_cross / jnp.sqrt(h_one * h_two)
    width = part_ref.shape[1]
    first = (lax.axis_index("z") * NC + lax.axis_index("core")) * count
    rows = pltpu.roll(part_ref[...], lax.rem(width - first, width), 1)
    roots = jnp.sqrt(jnp.concatenate([c_one, c_two], axis=0) / total)
    profiles_ref[...] = rows[:2, :count] / roots


def finish(part, sums, total, count):
    vmem = pl.BlockSpec(memory_space=pltpu.VMEM)
    return pl.pallas_call(
        functools.partial(finish_body, float(total), count),
        out_shape=(jax.ShapeDtypeStruct((2, count), jnp.float32), jax.ShapeDtypeStruct((1, 1), jnp.float32)),
        in_specs=[vmem, vmem],
        out_specs=(vmem, vmem),
        name="finish",
    )(part, sums)


def shards(layer_one, layer_two, spread):
    own = jnp.stack([layer_one, layer_two])
    count = own.shape[1]
    line = lax.all_gather(own, LINE, axis=1, tiled=True)
    near = [shift(own, 1, 0), shift(own, -1, 0), shift(own, 2, 0)]
    strip = jnp.concatenate([own] + near, axis=1)
    pieces = [strip, shift(strip, 0, 1), shift(strip, 0, -1), shift(strip, 0, 2)]
    part = line_sum(gram(spread, line, pieces))
    r_one, r_two = part[0], part[1]
    sums = jnp.stack([r_one, r_two, part[2], part[3], part[4], r_one * r_two, r_one * r_one, r_two * r_two])
    sums = plane_sum(jnp.sum(sums.reshape(8, part.shape[1] // 128, 128), axis=1))
    profiles, alignment = finish(part, sums, count * lax.axis_size(AXES), count)
    return (profiles, alignment.reshape(()))


def solution(mesh):
    finer = Mesh(mesh.devices.reshape(2, NZ, NY, NC, 2), AXES)
    return jax.shard_map(
        shards,
        mesh=finer,
        in_specs=(P(AXES, None), P(AXES, None), P()),
        out_specs=(P(None, AXES), P()),
        check_vma=False,
    )
```

```python
import functools
import math

import jax
import jax.numpy as jnp
from jax import lax
from jax.experimental import pallas as pl
from jax.experimental.pallas import tpu as pltpu
from jax.sharding import Mesh
from jax.sharding import PartitionSpec as P

D = 1024
AXES = ("x_hi", "z", "y", "core", "x_lo")
NX, NY, NZ, NC = (4, 4, 8, 2)
LOG2E = math.log2(math.e)


def linear(x, y, z, core):
    return (((x // 2 * NZ + z) * NY + y) * NC + core) * 2 + x % 2


def move(array, where):
    pairs = []
    for x in range(NX):
        for y in range(NY):
            for z in range(NZ):
                for core in range(NC):
                    tx, ty, tz, tcore = where(x, y, z, core)
                    pairs.append((linear(x, y, z, core), linear(tx % NX, ty % NY, tz % NZ, tcore % NC)))
    return lax.ppermute(array, AXES, pairs)


def shift(array, first, second):
    def where(x, y, z, core):
        dx, dy = (first, second) if core == 0 else (second, first)
        return x + dx, y + dy, z, core

    return move(array, where)


def fold_squares(rows):
    wide = rows.astype(jnp.float32)
    square = wide * wide
    folded = square[:, :128]
    for lane in range(128, D, 128):
        folded = folded + square[:, lane : lane + 128]
    return folded


def shuffled(array, moves, unit):
    lanes = lax.broadcasted_iota(jnp.int32, array.shape, 1)
    width = array.shape[1]
    result = array
    by_step = {}
    for old, fresh in moves.items():
        by_step.setdefault(fresh - old, []).append(fresh)
    for step, places in by_step.items():
        if step == 0:
            continue
        rolled = pltpu.roll(array, (step * unit) % width, 1)
        for place in places:
            inside = (lanes >= place * unit) & (lanes < (place + 1) * unit)
            result = jnp.where(inside, rolled, result)
    return result


def gram_body(n_line, spread_ref, *refs):
    line, pieces = refs[:n_line], refs[n_line:-3]
    out_ref, z_ref, norm_ref = refs[-3:]
    width = z_ref.shape[1]
    tall = pieces[0].shape[1]
    lanes = 128
    scales = [jnp.full((1, lanes), spread_ref[layer].astype(jnp.float32), jnp.float32) for layer in range(2)]
    factors = [LOG2E / scale for scale in scales]
    offsets = [jnp.exp(-D / scale) for scale in scales]
    at = 0
    for ref in line:
        z_ref[:, at : at + ref.shape[1], :] = ref[...]
        at += ref.shape[1]
    for index, piece in enumerate(pieces):
        for layer in range(2):
            norms = jnp.sum(fold_squares(piece[layer]), axis=1, keepdims=True)
            rows = slice(index * tall, (index + 1) * tall)
            norm_ref[layer, rows, :] = jnp.broadcast_to(norms, (tall, lanes)) * (0.5 * factors[layer])
    columns = []
    for start in range(0, width, lanes):
        z = [z_ref[layer, start : start + lanes, :] for layer in range(2)]
        z_norms = [
            jnp.sum(fold_squares(z[layer]).T, axis=0, keepdims=True) * (0.5 * factors[layer]) for layer in range(2)
        ]
        sums = [jnp.zeros((8, lanes), jnp.float32) for _ in range(5)]
        for index, piece in enumerate(pieces):
            kernels = []
            for layer in range(2):
                inner = lax.dot_general(
                    piece[layer], z[layer], (((1,), (1,)), ((), ())), preferred_element_type=jnp.float32
                )
                norms = norm_ref[layer, index * tall : (index + 1) * tall, :]
                kernels.append(jnp.exp2(inner * factors[layer] - norms - z_norms[layer]) - offsets[layer])
            one, two = kernels
            for row, term in enumerate((one, two, one * two, one * one, two * two)):
                sums[row] = sums[row] + jnp.sum(term.reshape(tall // 8, 8, lanes), axis=0)
        rows = [jnp.sum(term, axis=0, keepdims=True) for term in sums]
        columns.append(jnp.concatenate(rows + [jnp.zeros((3, lanes), jnp.float32)], axis=0))
    local = jnp.concatenate(columns, axis=1)
    count = width // (NZ * NC)
    other = {0: 1, 1: 0, 14: 15, 15: 14}
    other.update({place: place + 6 for place in range(2, 8)})
    other.update({place: place - 6 for place in range(8, 14)})
    local = jnp.where(lax.axis_index("core") == 0, local, shuffled(local, other, count))
    near = {0: 0, 1: 1, 2: 14, 3: 15, 4: 12, 5: 13, 6: 10, 7: 11, 8: 3, 9: 2, 10: 5, 11: 4, 12: 7, 13: 6, 14: 8, 15: 9}
    out_ref[...] = pltpu.roll(shuffled(local, near, count), lax.axis_index("z") * (NC * count), 1)


def gram(spread, line, pieces):
    vmem = pl.BlockSpec(memory_space=pltpu.VMEM)
    rows = sum(piece.shape[1] for piece in pieces)
    width = sum(part.shape[1] for part in line)
    return pl.pallas_call(
        functools.partial(gram_body, len(line)),
        out_shape=jax.ShapeDtypeStruct((8, width), jnp.float32),
        in_specs=[pl.BlockSpec(memory_space=pltpu.SMEM)] + [vmem] * (len(line) + len(pieces)),
        out_specs=vmem,
        scratch_shapes=[pltpu.VMEM((2, width, D), jnp.bfloat16), pltpu.VMEM((2, rows, 128), jnp.float32)],
        compiler_params=pltpu.CompilerParams(vmem_limit_bytes=24 << 20),
        cost_estimate=pl.CostEstimate(
            flops=4 * rows * width * D, bytes_accessed=4 * (rows + width) * D, transcendentals=2 * rows * width
        ),
        name="gram",
    )(spread, *line, *pieces)


def swap(array):
    return move(array, lambda x, y, z, core: (x, y, z, 1 - core))


def around(array):
    return move(array, lambda x, y, z, core: (x, y, z + 1 - 2 * core, core))


def line_sum(array):
    array = array + swap(array)
    for bit in (1, 2, 4):
        array = array + move(array, lambda x, y, z, core: (x, y, z ^ bit, core))
    return array


def plane_sum(array):
    for stage in range(2):
        parts = [shift(array, *((step, 0) if stage == 0 else (0, step))) for step in (1, -1, 2)]
        array = (array + parts[2]) + (parts[0] + parts[1])
    return 0.5 * (array + swap(array))


def finish_body(total, count, part_ref, sums_ref, profiles_ref, alignment_ref):
    sums = jnp.sum(sums_ref[...], axis=1, keepdims=True)
    sum_one, sum_two, f_cross, f_one, f_two, c_cross, c_one, c_two = (sums[at : at + 1, :] for at in range(8))
    h_cross = f_cross - 2.0 * c_cross / total + sum_one * sum_two / (total * total)
    h_one = f_one - 2.0 * c_one / total + sum_one * sum_one / (total * total)
    h_two = f_two - 2.0 * c_two / total + sum_two * sum_two / (total * total)
    alignment_ref[...] = h_cross / jnp.sqrt(h_one * h_two)
    width = part_ref.shape[1]
    first = (lax.axis_index("z") * NC + lax.axis_index("core")) * count
    rows = pltpu.roll(part_ref[...], lax.rem(width - first, width), 1)
    roots = jnp.sqrt(jnp.concatenate([c_one, c_two], axis=0) / total)
    profiles_ref[...] = rows[:2, :count] / roots


def finish(part, sums, total, count):
    vmem = pl.BlockSpec(memory_space=pltpu.VMEM)
    return pl.pallas_call(
        functools.partial(finish_body, float(total), count),
        out_shape=(jax.ShapeDtypeStruct((2, count), jnp.float32), jax.ShapeDtypeStruct((1, 1), jnp.float32)),
        in_specs=[vmem, vmem],
        out_specs=(vmem, vmem),
        name="finish",
    )(part, sums)


def shards(layer_one, layer_two, spread):
    own = jnp.stack([layer_one, layer_two])
    count = own.shape[1]
    chip = jnp.concatenate([own, swap(own)], axis=1)
    near = [shift(own, step, 0) for step in (1, -1, 2)]
    strip = jnp.concatenate([own] + near, axis=1)
    first, strip = lax.optimization_barrier((around(chip), strip))
    pieces = [strip] + [shift(strip, 0, step) for step in (1, -1, 2)]
    ring = [first]
    for _ in range(2):
        ring.append(around(ring[-1]))
    last = around(ring[-1][:, :count])
    pieces, late = lax.optimization_barrier((pieces, ring))
    ends = jnp.concatenate([last, swap(last)], axis=1)
    line = [chip] + ring + [swap(block) for block in late] + [ends]
    part = line_sum(gram(spread, line, pieces))
    r_one, r_two = part[0], part[1]
    sums = jnp.stack([r_one, r_two, part[2], part[3], part[4], r_one * r_two, r_one * r_one, r_two * r_two])
    sums = plane_sum(jnp.sum(sums.reshape(8, part.shape[1] // 128, 128), axis=1))
    profiles, alignment = finish(part, sums, count * lax.axis_size(AXES), count)
    return (profiles, alignment.reshape(()))


def solution(mesh):
    finer = Mesh(mesh.devices.reshape(2, NZ, NY, NC, 2), AXES)
    return jax.shard_map(
        shards,
        mesh=finer,
        in_specs=(P(AXES, None), P(AXES, None), P()),
        out_specs=(P(None, AXES), P()),
        check_vma=False,
    )
```

```python
import functools
import math

import jax
import jax.numpy as jnp
from jax import lax
from jax.experimental import pallas as pl
from jax.experimental.pallas import tpu as pltpu
from jax.sharding import Mesh
from jax.sharding import PartitionSpec as P

D = 1024
AXES = ("x_hi", "z", "y", "core", "x_lo")
NX, NY, NZ, NC = (4, 4, 8, 2)
LOG2E = math.log2(math.e)


def linear(x, y, z, core):
    return (((x // 2 * NZ + z) * NY + y) * NC + core) * 2 + x % 2


def move(array, where):
    pairs = []
    for x in range(NX):
        for y in range(NY):
            for z in range(NZ):
                for core in range(NC):
                    tx, ty, tz, tcore = where(x, y, z, core)
                    pairs.append((linear(x, y, z, core), linear(tx % NX, ty % NY, tz % NZ, tcore % NC)))
    return lax.ppermute(array, AXES, pairs)


def shift(array, first, second):
    def where(x, y, z, core):
        dx, dy = (first, second) if core == 0 else (second, first)
        return x + dx, y + dy, z, core

    return move(array, where)


def fold_squares(rows):
    wide = rows.astype(jnp.float32)
    square = wide * wide
    folded = square[:, :128]
    for lane in range(128, D, 128):
        folded = folded + square[:, lane : lane + 128]
    return folded


def shuffled(array, moves, unit):
    lanes = lax.broadcasted_iota(jnp.int32, array.shape, 1)
    width = array.shape[1]
    result = array
    by_step = {}
    for old, fresh in moves.items():
        by_step.setdefault(fresh - old, []).append(fresh)
    for step, places in by_step.items():
        if step == 0:
            continue
        rolled = pltpu.roll(array, (step * unit) % width, 1)
        for place in places:
            inside = (lanes >= place * unit) & (lanes < (place + 1) * unit)
            result = jnp.where(inside, rolled, result)
    return result


def gram_body(n_line, spread_ref, *refs):
    line, pieces = refs[:n_line], refs[n_line:-4]
    out_ref, z_ref, w_ref, norm_ref = refs[-4:]
    width = z_ref.shape[1]
    tall = pieces[0].shape[1]
    scales = [jnp.full((1, 128), spread_ref[layer].astype(jnp.float32), jnp.float32) for layer in range(2)]
    factors = [LOG2E / scale for scale in scales]
    offsets = [jnp.exp(-D / scale) for scale in scales]
    at = 0
    for ref in line:
        z_ref[:, at : at + ref.shape[1], :] = ref[...]
        at += ref.shape[1]
    for index, piece in enumerate(pieces):
        rows = slice(index * tall, (index + 1) * tall)
        for layer in range(2):
            block = piece[layer]
            w_ref[layer, rows, :] = block
            norms = jnp.sum(fold_squares(block), axis=1, keepdims=True)
            norm_ref[layer, rows, :] = jnp.broadcast_to(norms, (tall, 128)) * (0.5 * factors[layer])
    columns = []
    height = w_ref.shape[1] // 2
    for start in range(0, width, 256):
        spans = range(start, min(start + 256, width), 128)
        wide = lambda row: jnp.concatenate([row] * len(spans), axis=1)
        z_norms = []
        for layer in range(2):
            norms = [
                jnp.sum(fold_squares(z_ref[layer, span : span + 128, :]).T, axis=0, keepdims=True) for span in spans
            ]
            z_norms.append(jnp.concatenate(norms, axis=1) * (0.5 * wide(factors[layer])))
        lanes = 128 * len(spans)
        sums = [jnp.zeros((8, lanes), jnp.float32) for _ in range(5)]
        for top in range(0, w_ref.shape[1], height):
            kernels = []
            for layer in range(2):
                inner = lax.dot_general(
                    w_ref[layer, top : top + height, :],
                    z_ref[layer, start : start + lanes, :],
                    (((1,), (1,)), ((), ())),
                    preferred_element_type=jnp.float32,
                )
                power = inner * wide(factors[layer]) - wide(norm_ref[layer, top : top + height, :]) - z_norms[layer]
                kernels.append(jnp.exp2(power) - wide(offsets[layer]))
            one, two = kernels
            for row, term in enumerate((one, two, one * two, one * one, two * two)):
                sums[row] = sums[row] + jnp.sum(term.reshape(height // 8, 8, lanes), axis=0)
        rows = [jnp.sum(term, axis=0, keepdims=True) for term in sums]
        columns.append(jnp.concatenate(rows + [jnp.zeros((3, lanes), jnp.float32)], axis=0))
    local = jnp.concatenate(columns, axis=1)
    count = width // (NZ * NC)
    other = {0: 1, 1: 0, 14: 15, 15: 14}
    other.update({place: place + 6 for place in range(2, 8)})
    other.update({place: place - 6 for place in range(8, 14)})
    local = jnp.where(lax.axis_index("core") == 0, local, shuffled(local, other, count))
    near = {0: 0, 1: 1, 2: 14, 3: 15, 4: 12, 5: 13, 6: 10, 7: 11, 8: 3, 9: 2, 10: 5, 11: 4, 12: 7, 13: 6, 14: 8, 15: 9}
    out_ref[...] = pltpu.roll(shuffled(local, near, count), lax.axis_index("z") * (NC * count), 1)


def gram(spread, line, pieces):
    vmem = pl.BlockSpec(memory_space=pltpu.VMEM)
    rows = sum(piece.shape[1] for piece in pieces)
    width = sum(part.shape[1] for part in line)
    return pl.pallas_call(
        functools.partial(gram_body, len(line)),
        out_shape=jax.ShapeDtypeStruct((8, width), jnp.float32),
        in_specs=[pl.BlockSpec(memory_space=pltpu.SMEM)] + [vmem] * (len(line) + len(pieces)),
        out_specs=vmem,
        scratch_shapes=[
            pltpu.VMEM((2, width, D), jnp.bfloat16),
            pltpu.VMEM((2, rows, D), jnp.bfloat16),
            pltpu.VMEM((2, rows, 128), jnp.float32),
        ],
        compiler_params=pltpu.CompilerParams(vmem_limit_bytes=24 << 20),
        cost_estimate=pl.CostEstimate(
            flops=4 * rows * width * D, bytes_accessed=4 * (rows + width) * D, transcendentals=2 * rows * width
        ),
        name="gram",
    )(spread, *line, *pieces)


def swap(array):
    return move(array, lambda x, y, z, core: (x, y, z, 1 - core))


def around(array):
    return move(array, lambda x, y, z, core: (x, y, z + 1 - 2 * core, core))


def line_sum(array):
    array = array + swap(array)
    for bit in (1, 2, 4):
        array = array + move(array, lambda x, y, z, core: (x, y, z ^ bit, core))
    return array


def plane_sum(array):
    for stage in range(2):
        parts = [shift(array, *((step, 0) if stage == 0 else (0, step))) for step in (1, -1, 2)]
        array = (array + parts[2]) + (parts[0] + parts[1])
    return 0.5 * (array + swap(array))


def finish_body(total, count, part_ref, sums_ref, profiles_ref, alignment_ref):
    sums = jnp.sum(sums_ref[...], axis=1, keepdims=True)
    sum_one, sum_two, f_cross, f_one, f_two, c_cross, c_one, c_two = (sums[at : at + 1, :] for at in range(8))
    h_cross = f_cross - 2.0 * c_cross / total + sum_one * sum_two / (total * total)
    h_one = f_one - 2.0 * c_one / total + sum_one * sum_one / (total * total)
    h_two = f_two - 2.0 * c_two / total + sum_two * sum_two / (total * total)
    alignment_ref[...] = h_cross / jnp.sqrt(h_one * h_two)
    width = part_ref.shape[1]
    first = (lax.axis_index("z") * NC + lax.axis_index("core")) * count
    rows = pltpu.roll(part_ref[...], lax.rem(width - first, width), 1)
    roots = jnp.sqrt(jnp.concatenate([c_one, c_two], axis=0) / total)
    profiles_ref[...] = rows[:2, :count] / roots


def finish(part, sums, total, count):
    vmem = pl.BlockSpec(memory_space=pltpu.VMEM)
    return pl.pallas_call(
        functools.partial(finish_body, float(total), count),
        out_shape=(jax.ShapeDtypeStruct((2, count), jnp.float32), jax.ShapeDtypeStruct((1, 1), jnp.float32)),
        in_specs=[vmem, vmem],
        out_specs=(vmem, vmem),
        name="finish",
    )(part, sums)


def shards(layer_one, layer_two, spread):
    own = lax.optimization_barrier(jnp.stack([layer_one, layer_two]))
    count = own.shape[1]
    near = [shift(own, step, 0) for step in (1, -1, 2)]
    chip = jnp.concatenate([own, swap(own)], axis=1)
    strip = jnp.concatenate([own] + near, axis=1)
    first, strip = lax.optimization_barrier((around(chip), strip))
    pieces = [strip] + [shift(strip, 0, step) for step in (1, -1, 2)]
    ring = [first]
    for _ in range(2):
        ring.append(around(ring[-1]))
    last = around(ring[2][:, :count])
    pieces, late = lax.optimization_barrier((pieces, last))
    ends = jnp.concatenate([last, swap(late)], axis=1)
    line = [chip] + ring + [swap(block) for block in ring] + [ends]
    part = line_sum(gram(spread, line, pieces))
    r_one, r_two = part[0], part[1]
    sums = jnp.stack([r_one, r_two, part[2], part[3], part[4], r_one * r_two, r_one * r_one, r_two * r_two])
    sums = plane_sum(jnp.sum(sums.reshape(8, part.shape[1] // 128, 128), axis=1))
    profiles, alignment = finish(part, sums, count * lax.axis_size(AXES), count)
    return (profiles, alignment.reshape(()))


def solution(mesh):
    finer = Mesh(mesh.devices.reshape(2, NZ, NY, NC, 2), AXES)
    return jax.shard_map(
        shards,
        mesh=finer,
        in_specs=(P(AXES, None), P(AXES, None), P()),
        out_specs=(P(None, AXES), P()),
        check_vma=False,
    )
```

```python
import functools
import math

import jax
import jax.numpy as jnp
from jax import lax
from jax.experimental import pallas as pl
from jax.experimental.pallas import tpu as pltpu
from jax.sharding import Mesh
from jax.sharding import PartitionSpec as P

D = 1024
AXES = ("x_hi", "z", "y", "core", "x_lo")
NX, NY, NZ, NC = (4, 4, 8, 2)
LOG2E = math.log2(math.e)


def linear(x, y, z, core):
    return (((x // 2 * NZ + z) * NY + y) * NC + core) * 2 + x % 2


def move(array, where):
    pairs = []
    for x in range(NX):
        for y in range(NY):
            for z in range(NZ):
                for core in range(NC):
                    tx, ty, tz, tcore = where(x, y, z, core)
                    pairs.append((linear(x, y, z, core), linear(tx % NX, ty % NY, tz % NZ, tcore % NC)))
    return lax.ppermute(array, AXES, pairs)


def shift(array, first, second):
    def where(x, y, z, core):
        dx, dy = (first, second) if core == 0 else (second, first)
        return x + dx, y + dy, z, core

    return move(array, where)


def fold_squares(rows):
    wide = rows.astype(jnp.float32)
    square = wide * wide
    folded = square[:, :128]
    for lane in range(128, D, 128):
        folded = folded + square[:, lane : lane + 128]
    return folded


def shuffled(array, moves, unit):
    lanes = lax.broadcasted_iota(jnp.int32, array.shape, 1)
    width = array.shape[1]
    result = array
    by_step = {}
    for old, fresh in moves.items():
        by_step.setdefault(fresh - old, []).append(fresh)
    for step, places in by_step.items():
        if step == 0:
            continue
        rolled = pltpu.roll(array, (step * unit) % width, 1)
        for place in places:
            inside = (lanes >= place * unit) & (lanes < (place + 1) * unit)
            result = jnp.where(inside, rolled, result)
    return result


def gram_body(n_line, spread_ref, *refs):
    line, pieces = refs[:n_line], refs[n_line:-4]
    out_ref, z_ref, w_ref, norm_ref = refs[-4:]
    width = z_ref.shape[1]
    tall = pieces[0].shape[1]
    scales = [jnp.full((1, 128), spread_ref[layer].astype(jnp.float32), jnp.float32) for layer in range(2)]
    factors = [LOG2E / scale for scale in scales]
    offsets = [jnp.exp(-D / scale) for scale in scales]
    at = 0
    for ref in line:
        z_ref[:, at : at + ref.shape[1], :] = ref[...]
        at += ref.shape[1]
    for index, piece in enumerate(pieces):
        rows = slice(index * tall, (index + 1) * tall)
        for layer in range(2):
            block = piece[layer]
            w_ref[layer, rows, :] = block
            norms = jnp.sum(fold_squares(block), axis=1, keepdims=True)
            norm_ref[layer, rows, :] = jnp.broadcast_to(norms, (tall, 128)) * (0.5 * factors[layer])
    columns = []
    height = w_ref.shape[1] // 2
    for start in range(0, width, 256):
        spans = range(start, min(start + 256, width), 128)
        wide = lambda row: jnp.concatenate([row] * len(spans), axis=1)
        z_norms = []
        for layer in range(2):
            norms = [
                jnp.sum(fold_squares(z_ref[layer, span : span + 128, :]).T, axis=0, keepdims=True) for span in spans
            ]
            z_norms.append(jnp.concatenate(norms, axis=1) * (0.5 * wide(factors[layer])))
        lanes = 128 * len(spans)
        sums = [jnp.zeros((8, lanes), jnp.float32) for _ in range(5)]
        for top in range(0, w_ref.shape[1], height):
            kernels = []
            for layer in range(2):
                inner = lax.dot_general(
                    w_ref[layer, top : top + height, :],
                    z_ref[layer, start : start + lanes, :],
                    (((1,), (1,)), ((), ())),
                    preferred_element_type=jnp.float32,
                )
                power = inner * wide(factors[layer]) - wide(norm_ref[layer, top : top + height, :]) - z_norms[layer]
                kernels.append(jnp.exp2(power) - wide(offsets[layer]))
            one, two = kernels
            for row, term in enumerate((one, two, one * two, one * one, two * two)):
                sums[row] = sums[row] + jnp.sum(term.reshape(height // 8, 8, lanes), axis=0)
        rows = [jnp.sum(term, axis=0, keepdims=True) for term in sums]
        columns.append(jnp.concatenate(rows + [jnp.zeros((3, lanes), jnp.float32)], axis=0))
    local = jnp.concatenate(columns, axis=1)
    count = width // (NZ * NC)
    other = {0: 1, 1: 0, 14: 15, 15: 14}
    other.update({place: place + 6 for place in range(2, 8)})
    other.update({place: place - 6 for place in range(8, 14)})
    local = jnp.where(lax.axis_index("core") == 0, local, shuffled(local, other, count))
    near = {0: 0, 1: 1, 2: 14, 3: 15, 4: 12, 5: 13, 6: 10, 7: 11, 8: 3, 9: 2, 10: 5, 11: 4, 12: 7, 13: 6, 14: 8, 15: 9}
    out_ref[...] = pltpu.roll(shuffled(local, near, count), lax.axis_index("z") * (NC * count), 1)


def gram(spread, line, pieces):
    vmem = pl.BlockSpec(memory_space=pltpu.VMEM)
    rows = sum(piece.shape[1] for piece in pieces)
    width = sum(part.shape[1] for part in line)
    return pl.pallas_call(
        functools.partial(gram_body, len(line)),
        out_shape=jax.ShapeDtypeStruct((8, width), jnp.float32),
        in_specs=[pl.BlockSpec(memory_space=pltpu.SMEM)] + [vmem] * (len(line) + len(pieces)),
        out_specs=vmem,
        scratch_shapes=[
            pltpu.VMEM((2, width, D), jnp.bfloat16),
            pltpu.VMEM((2, rows, D), jnp.bfloat16),
            pltpu.VMEM((2, rows, 128), jnp.float32),
        ],
        compiler_params=pltpu.CompilerParams(vmem_limit_bytes=24 << 20),
        cost_estimate=pl.CostEstimate(
            flops=4 * rows * width * D, bytes_accessed=4 * (rows + width) * D, transcendentals=2 * rows * width
        ),
        name="gram",
    )(spread, *line, *pieces)


def swap(array):
    return move(array, lambda x, y, z, core: (x, y, z, 1 - core))


def around(array):
    return move(array, lambda x, y, z, core: (x, y, z + 1 - 2 * core, core))


def line_sum(array):
    array = array + swap(array)
    array = array + move(array, lambda x, y, z, core: (x, y, z ^ 1, core))
    parts = [move(array, lambda x, y, z, core: (x, y, z + step, core)) for step in (2, -2, 4)]
    return ring_sum(array, parts)


def ring_parts(array, axis):
    return [
        move(array, lambda x, y, z, core: (x + step, y, z, core) if axis == "x" else (x, y + step, z, core))
        for step in (1, -1, 2)
    ]


def ring_sum(array, parts):
    return (array + parts[2]) + (parts[0] + parts[1])


def finish_body(total, count, part_ref, sums_ref, *refs):
    parts, (profiles_ref, alignment_ref) = refs[:3], refs[3:]
    sums = jnp.sum(ring_sum(sums_ref[...], [part[...] for part in parts]), axis=1, keepdims=True)
    sum_one, sum_two, f_cross, f_one, f_two, c_cross, c_one, c_two = (sums[at : at + 1, :] for at in range(8))
    h_cross = f_cross - 2.0 * c_cross / total + sum_one * sum_two / (total * total)
    h_one = f_one - 2.0 * c_one / total + sum_one * sum_one / (total * total)
    h_two = f_two - 2.0 * c_two / total + sum_two * sum_two / (total * total)
    alignment_ref[...] = h_cross / jnp.sqrt(h_one * h_two)
    width = part_ref.shape[1]
    first = (lax.axis_index("z") * NC + lax.axis_index("core")) * count
    rows = pltpu.roll(part_ref[...], lax.rem(width - first, width), 1)
    roots = jnp.sqrt(jnp.concatenate([c_one, c_two], axis=0) / total)
    profiles_ref[...] = rows[:2, :count] / roots


def finish(part, sums, parts, total, count):
    vmem = pl.BlockSpec(memory_space=pltpu.VMEM)
    return pl.pallas_call(
        functools.partial(finish_body, float(total), count),
        out_shape=(jax.ShapeDtypeStruct((2, count), jnp.float32), jax.ShapeDtypeStruct((1, 1), jnp.float32)),
        in_specs=[vmem] * 5,
        out_specs=(vmem, vmem),
        compiler_params=pltpu.CompilerParams(vmem_limit_bytes=2 << 20),
        name="finish",
    )(part, sums, *parts)


def shards(layer_one, layer_two, spread):
    own = lax.optimization_barrier(jnp.stack([layer_one, layer_two]))
    count = own.shape[1]
    near = [shift(own, step, 0) for step in (1, -1, 2)]
    chip = jnp.concatenate([own, swap(own)], axis=1)
    strip = jnp.concatenate([own] + near, axis=1)
    first, strip = lax.optimization_barrier((around(chip), strip))
    pieces = [strip] + [shift(strip, 0, step) for step in (1, -1, 2)]
    ring = [first]
    for _ in range(2):
        ring.append(around(ring[-1]))
    last = around(ring[2][:, :count])
    pieces, late = lax.optimization_barrier((pieces, last))
    ends = jnp.concatenate([last, swap(late)], axis=1)
    line = [chip] + ring + [swap(block) for block in ring] + [ends]
    part = line_sum(gram(spread, line, pieces))
    r_one, r_two = part[0], part[1]
    sums = jnp.stack([r_one, r_two, part[2], part[3], part[4], r_one * r_two, r_one * r_one, r_two * r_two])
    sums = jnp.sum(sums.reshape(8, part.shape[1] // 128, 128), axis=1)
    sums = ring_sum(sums, ring_parts(sums, "x"))
    profiles, alignment = finish(part, sums, ring_parts(sums, "y"), count * lax.axis_size(AXES), count)
    return (profiles, alignment.reshape(()))


def solution(mesh):
    finer = Mesh(mesh.devices.reshape(2, NZ, NY, NC, 2), AXES)
    return jax.shard_map(
        shards,
        mesh=finer,
        in_specs=(P(AXES, None), P(AXES, None), P()),
        out_specs=(P(None, AXES), P()),
        check_vma=False,
    )
```

```python
import functools
import math

import jax
import jax.numpy as jnp
from jax import lax
from jax.experimental import pallas as pl
from jax.experimental.pallas import tpu as pltpu
from jax.sharding import Mesh
from jax.sharding import PartitionSpec as P

D = 1024
AXES = ("x_hi", "z", "y", "core", "x_lo")
NX, NY, NZ, NC = (4, 4, 8, 2)
LOG2E = math.log2(math.e)


def linear(x, y, z, core):
    return (((x // 2 * NZ + z) * NY + y) * NC + core) * 2 + x % 2


def move(array, where):
    pairs = []
    for x in range(NX):
        for y in range(NY):
            for z in range(NZ):
                for core in range(NC):
                    tx, ty, tz, tcore = where(x, y, z, core)
                    pairs.append((linear(x, y, z, core), linear(tx % NX, ty % NY, tz % NZ, tcore % NC)))
    return lax.ppermute(array, AXES, pairs)


def shift(array, first, second):
    def where(x, y, z, core):
        dx, dy = (first, second) if core == 0 else (second, first)
        return x + dx, y + dy, z, core

    return move(array, where)


def fold_squares(rows):
    wide = rows.astype(jnp.float32)
    square = wide * wide
    folded = square[:, :128]
    for lane in range(128, D, 128):
        folded = folded + square[:, lane : lane + 128]
    return folded


def shuffled(array, moves, unit):
    lanes = lax.broadcasted_iota(jnp.int32, array.shape, 1)
    width = array.shape[1]
    result = array
    by_step = {}
    for old, fresh in moves.items():
        by_step.setdefault(fresh - old, []).append(fresh)
    for step, places in by_step.items():
        if step == 0:
            continue
        rolled = pltpu.roll(array, (step * unit) % width, 1)
        for place in places:
            inside = (lanes >= place * unit) & (lanes < (place + 1) * unit)
            result = jnp.where(inside, rolled, result)
    return result


def plane_body(spread_ref, *refs):
    pieces, (w_ref, norm_ref) = refs[:-2], refs[-2:]
    tall = pieces[0].shape[1]
    for layer in range(2):
        factor = LOG2E / jnp.full((1, 128), spread_ref[layer].astype(jnp.float32), jnp.float32)
        for index, piece in enumerate(pieces):
            rows = slice(index * tall, (index + 1) * tall)
            block = piece[layer]
            w_ref[layer, rows, :] = block
            norms = jnp.sum(fold_squares(block), axis=1, keepdims=True)
            norm_ref[layer, rows, :] = jnp.broadcast_to(norms, (tall, 128)) * (0.5 * factor)


def plane_rows(spread, pieces):
    vmem = pl.BlockSpec(memory_space=pltpu.VMEM)
    rows = sum(piece.shape[1] for piece in pieces)
    return pl.pallas_call(
        plane_body,
        out_shape=(
            jax.ShapeDtypeStruct((2, rows, D), jnp.bfloat16),
            jax.ShapeDtypeStruct((2, rows, 128), jnp.float32),
        ),
        in_specs=[pl.BlockSpec(memory_space=pltpu.SMEM)] + [vmem] * len(pieces),
        out_specs=(vmem, vmem),
        compiler_params=pltpu.CompilerParams(vmem_limit_bytes=16 << 20),
        cost_estimate=pl.CostEstimate(flops=4 * rows * D, bytes_accessed=8 * rows * D, transcendentals=0),
        name="plane_rows",
    )(spread, *pieces)


def gram_body(spread_ref, w_ref, norm_ref, *refs):
    line, (out_ref, z_ref) = refs[:-2], refs[-2:]
    width = z_ref.shape[1]
    scales = [jnp.full((1, 128), spread_ref[layer].astype(jnp.float32), jnp.float32) for layer in range(2)]
    factors = [LOG2E / scale for scale in scales]
    offsets = [jnp.exp(-D / scale) for scale in scales]
    at = 0
    for ref in line:
        z_ref[:, at : at + ref.shape[1], :] = ref[...]
        at += ref.shape[1]
    columns = []
    height = w_ref.shape[1] // 2
    for start in range(0, width, 256):
        spans = range(start, min(start + 256, width), 128)
        wide = lambda row: jnp.concatenate([row] * len(spans), axis=1)
        z_norms = []
        for layer in range(2):
            norms = [
                jnp.sum(fold_squares(z_ref[layer, span : span + 128, :]).T, axis=0, keepdims=True) for span in spans
            ]
            z_norms.append(jnp.concatenate(norms, axis=1) * (0.5 * wide(factors[layer])))
        lanes = 128 * len(spans)
        sums = [jnp.zeros((8, lanes), jnp.float32) for _ in range(5)]
        for top in range(0, w_ref.shape[1], height):
            kernels = []
            for layer in range(2):
                inner = lax.dot_general(
                    w_ref[layer, top : top + height, :],
                    z_ref[layer, start : start + lanes, :],
                    (((1,), (1,)), ((), ())),
                    preferred_element_type=jnp.float32,
                )
                power = inner * wide(factors[layer]) - wide(norm_ref[layer, top : top + height, :]) - z_norms[layer]
                kernels.append(jnp.exp2(power) - wide(offsets[layer]))
            one, two = kernels
            for row, term in enumerate((one, two, one * two, one * one, two * two)):
                sums[row] = sums[row] + jnp.sum(term.reshape(height // 8, 8, lanes), axis=0)
        rows = [jnp.sum(term, axis=0, keepdims=True) for term in sums]
        columns.append(jnp.concatenate(rows + [jnp.zeros((3, lanes), jnp.float32)], axis=0))
    local = jnp.concatenate(columns, axis=1)
    count = width // (NZ * NC)
    other = {0: 1, 1: 0, 14: 15, 15: 14}
    other.update({place: place + 6 for place in range(2, 8)})
    other.update({place: place - 6 for place in range(8, 14)})
    local = jnp.where(lax.axis_index("core") == 0, local, shuffled(local, other, count))
    near = {0: 0, 1: 1, 2: 14, 3: 15, 4: 12, 5: 13, 6: 10, 7: 11, 8: 3, 9: 2, 10: 5, 11: 4, 12: 7, 13: 6, 14: 8, 15: 9}
    local = pltpu.roll(shuffled(local, near, count), lax.axis_index("z") * (NC * count), 1)
    parts = [local[:, start : start + 128] for start in range(0, width, 128)]
    folded = functools.reduce(lambda total, part: total + part, parts)
    for index, part in enumerate(parts):
        out_ref[index : index + 1, :] = part[0:1]
        out_ref[8 + index : 9 + index, :] = part[1:2]
    out_ref[7:8, :] = folded[2:3]
    halves = folded + pltpu.roll(folded, 64, 1)
    left = lax.broadcasted_iota(jnp.int32, (1, 128), 1) < 64
    out_ref[15:16, :] = jnp.where(left, halves[3:4], halves[4:5])


def gram(spread, columns, norms, line):
    vmem = pl.BlockSpec(memory_space=pltpu.VMEM)
    rows = columns.shape[1]
    width = sum(part.shape[1] for part in line)
    return pl.pallas_call(
        gram_body,
        out_shape=jax.ShapeDtypeStruct((16, 128), jnp.float32),
        in_specs=[pl.BlockSpec(memory_space=pltpu.SMEM)] + [vmem] * (2 + len(line)),
        out_specs=vmem,
        scratch_shapes=[pltpu.VMEM((2, width, D), jnp.bfloat16)],
        compiler_params=pltpu.CompilerParams(vmem_limit_bytes=20 << 20),
        cost_estimate=pl.CostEstimate(
            flops=4 * rows * width * D, bytes_accessed=4 * (rows + width) * D, transcendentals=2 * rows * width
        ),
        name="gram",
    )(spread, columns, norms, *line)


def swap(array):
    return move(array, lambda x, y, z, core: (x, y, z, 1 - core))


def around(array):
    return move(array, lambda x, y, z, core: (x, y, z + 1 - 2 * core, core))


def line_sum(array):
    array = array + swap(array)
    array = array + move(array, lambda x, y, z, core: (x, y, z ^ 1, core))
    parts = [move(array, lambda x, y, z, core: (x, y, z + step, core)) for step in (2, -2, 4)]
    return ring_sum(array, parts)


def ring_parts(array, axis):
    return [
        move(array, lambda x, y, z, core: (x + step, y, z, core) if axis == "x" else (x, y + step, z, core))
        for step in (1, -1, 2)
    ]


def ring_sum(array, parts):
    return (array + parts[2]) + (parts[0] + parts[1])


def finish_body(total, count, part_ref, sums_ref, *refs):
    parts, (profiles_ref, alignment_ref) = refs[:3], refs[3:]
    lanes = ring_sum(sums_ref[...], [part[...] for part in parts])
    sums = jnp.sum(lanes, axis=1, keepdims=True)
    sum_one, sum_two, f_cross, _, c_cross, c_one, c_two = (sums[at : at + 1, :] for at in range(7))
    left = lax.broadcasted_iota(jnp.int32, (1, 128), 1) < 64
    f_one = jnp.sum(jnp.where(left, lanes[3:4], 0.0), axis=1, keepdims=True)
    f_two = jnp.sum(jnp.where(left, 0.0, lanes[3:4]), axis=1, keepdims=True)
    h_cross = f_cross - 2.0 * c_cross / total + sum_one * sum_two / (total * total)
    h_one = f_one - 2.0 * c_one / total + sum_one * sum_one / (total * total)
    h_two = f_two - 2.0 * c_two / total + sum_two * sum_two / (total * total)
    alignment_ref[...] = h_cross / jnp.sqrt(h_one * h_two)
    width = NZ * NC * count
    first = (lax.axis_index("z") * NC + lax.axis_index("core")) * count
    for layer, c_sum in enumerate((c_one, c_two)):
        rows = jnp.concatenate([part_ref[8 * layer + at : 8 * layer + at + 1, :] for at in range(7)], axis=1)
        rows = pltpu.roll(jnp.broadcast_to(rows, (8, width)), lax.rem(width - first, width), 1)
        profiles_ref[layer : layer + 1, :] = rows[:1, :count] / jnp.sqrt(c_sum / total)


def finish(part, sums, parts, total, count):
    vmem = pl.BlockSpec(memory_space=pltpu.VMEM)
    return pl.pallas_call(
        functools.partial(finish_body, float(total), count),
        out_shape=(jax.ShapeDtypeStruct((2, count), jnp.float32), jax.ShapeDtypeStruct((1, 1), jnp.float32)),
        in_specs=[vmem] * 5,
        out_specs=(vmem, vmem),
        compiler_params=pltpu.CompilerParams(vmem_limit_bytes=2 << 20),
        name="finish",
    )(part, sums, *parts)


def shards(layer_one, layer_two, spread):
    own = lax.optimization_barrier(jnp.stack([layer_one, layer_two]))
    count = own.shape[1]
    near = [shift(own, step, 0) for step in (1, -1, 2)]
    chip = jnp.concatenate([own, swap(own)], axis=1)
    strip = jnp.concatenate([own] + near, axis=1)
    first, strip = lax.optimization_barrier((around(chip), strip))
    pieces = [strip] + [shift(strip, 0, step) for step in (1, -1, 2)]
    ring = [first]
    for _ in range(2):
        ring.append(around(ring[-1]))
    last = around(ring[2][:, :count])
    ends = jnp.concatenate([last, swap(last)], axis=1)
    line = [chip] + ring + [swap(block) for block in ring] + [ends]
    part = line_sum(gram(spread, *plane_rows(spread, pieces), line))
    r_one, r_two = part[0:7], part[8:15]
    terms = [r_one, r_two, part[7:8], part[15:16], r_one * r_two, r_one * r_one, r_two * r_two]
    sums = jnp.stack([jnp.sum(term, axis=0) for term in terms] + [jnp.zeros((128,), jnp.float32)])
    sums = ring_sum(sums, ring_parts(sums, "x"))
    profiles, alignment = finish(part, sums, ring_parts(sums, "y"), count * lax.axis_size(AXES), count)
    return (profiles, alignment.reshape(()))


def solution(mesh):
    finer = Mesh(mesh.devices.reshape(2, NZ, NY, NC, 2), AXES)
    return jax.shard_map(
        shards,
        mesh=finer,
        in_specs=(P(AXES, None), P(AXES, None), P()),
        out_specs=(P(None, AXES), P()),
        check_vma=False,
    )
```

```python
import functools
import math

import jax
import jax.numpy as jnp
from jax import lax
from jax.experimental import pallas as pl
from jax.experimental.pallas import tpu as pltpu
from jax.sharding import Mesh
from jax.sharding import PartitionSpec as P

D = 1024
AXES = ("x_hi", "z", "y", "core", "x_lo")
NX, NY, NZ, NC = (4, 4, 8, 2)
LOG2E = math.log2(math.e)


def linear(x, y, z, core):
    return (((x // 2 * NZ + z) * NY + y) * NC + core) * 2 + x % 2


def move(array, where):
    pairs = []
    for x in range(NX):
        for y in range(NY):
            for z in range(NZ):
                for core in range(NC):
                    tx, ty, tz, tcore = where(x, y, z, core)
                    pairs.append((linear(x, y, z, core), linear(tx % NX, ty % NY, tz % NZ, tcore % NC)))
    return lax.ppermute(array, AXES, pairs)


def shift(array, first, second):
    def where(x, y, z, core):
        dx, dy = (first, second) if core == 0 else (second, first)
        return x + dx, y + dy, z, core

    return move(array, where)


def fold_squares(rows):
    wide = rows.astype(jnp.float32)
    square = wide * wide
    folded = square[:, :128]
    for lane in range(128, D, 128):
        folded = folded + square[:, lane : lane + 128]
    return folded


def shuffled(array, moves, unit):
    lanes = lax.broadcasted_iota(jnp.int32, array.shape, 1)
    width = array.shape[1]
    result = array
    by_step = {}
    for old, fresh in moves.items():
        by_step.setdefault(fresh - old, []).append(fresh)
    for step, places in by_step.items():
        if step == 0:
            continue
        rolled = pltpu.roll(array, (step * unit) % width, 1)
        for place in places:
            inside = (lanes >= place * unit) & (lanes < (place + 1) * unit)
            result = jnp.where(inside, rolled, result)
    return result


def plane_body(spread_ref, *refs):
    pieces, (w_ref, norm_ref) = refs[:-2], refs[-2:]
    tall = pieces[0].shape[1]
    for layer in range(2):
        factor = LOG2E / jnp.full((1, 128), spread_ref[layer].astype(jnp.float32), jnp.float32)
        for index, piece in enumerate(pieces):
            rows = slice(index * tall, (index + 1) * tall)
            block = piece[layer]
            w_ref[layer, rows, :] = block
            norms = jnp.sum(fold_squares(block), axis=1, keepdims=True)
            norm_ref[layer, rows, :] = jnp.broadcast_to(norms, (tall, 128)) * (0.5 * factor)


def plane_rows(spread, pieces):
    vmem = pl.BlockSpec(memory_space=pltpu.VMEM)
    rows = sum(piece.shape[1] for piece in pieces)
    return pl.pallas_call(
        plane_body,
        out_shape=(
            jax.ShapeDtypeStruct((2, rows, D), jnp.bfloat16),
            jax.ShapeDtypeStruct((2, rows, 128), jnp.float32),
        ),
        in_specs=[pl.BlockSpec(memory_space=pltpu.SMEM)] + [vmem] * len(pieces),
        out_specs=(vmem, vmem),
        compiler_params=pltpu.CompilerParams(vmem_limit_bytes=16 << 20),
        cost_estimate=pl.CostEstimate(flops=4 * rows * D, bytes_accessed=8 * rows * D, transcendentals=0),
        name="plane_rows",
    )(spread, *pieces)


def gram_body(spread_ref, w_ref, norm_ref, *refs):
    line, (out_ref, z_ref) = refs[:-2], refs[-2:]
    width = z_ref.shape[1]
    scales = [jnp.full((1, 128), spread_ref[layer].astype(jnp.float32), jnp.float32) for layer in range(2)]
    factors = [LOG2E / scale for scale in scales]
    offsets = [jnp.exp(-D / scale) for scale in scales]
    at = 0
    for ref in line:
        z_ref[:, at : at + ref.shape[1], :] = ref[...]
        at += ref.shape[1]
    columns = []
    height = w_ref.shape[1] // 2
    for start in range(0, width, 256):
        spans = range(start, min(start + 256, width), 128)
        wide = lambda row: jnp.concatenate([row] * len(spans), axis=1)
        z_norms = []
        for layer in range(2):
            norms = [
                jnp.sum(fold_squares(z_ref[layer, span : span + 128, :]).T, axis=0, keepdims=True) for span in spans
            ]
            z_norms.append(jnp.concatenate(norms, axis=1) * (0.5 * wide(factors[layer])))
        lanes = 128 * len(spans)
        sums = [jnp.zeros((8, lanes), jnp.float32) for _ in range(5)]
        for top in range(0, w_ref.shape[1], height):
            kernels = []
            for layer in range(2):
                inner = lax.dot_general(
                    w_ref[layer, top : top + height, :],
                    z_ref[layer, start : start + lanes, :],
                    (((1,), (1,)), ((), ())),
                    preferred_element_type=jnp.float32,
                )
                power = inner * wide(factors[layer]) - wide(norm_ref[layer, top : top + height, :]) - z_norms[layer]
                kernels.append(jnp.exp2(power) - wide(offsets[layer]))
            one, two = kernels
            for row, term in enumerate((one, two, one * two, one * one, two * two)):
                sums[row] = sums[row] + jnp.sum(term.reshape(height // 8, 8, lanes), axis=0)
        rows = [jnp.sum(term, axis=0, keepdims=True) for term in sums]
        columns.append(jnp.concatenate(rows + [jnp.zeros((3, lanes), jnp.float32)], axis=0))
    local = jnp.concatenate(columns, axis=1)
    count = width // (NZ * NC)
    other = {0: 1, 1: 0, 14: 15, 15: 14}
    other.update({place: place + 6 for place in range(2, 8)})
    other.update({place: place - 6 for place in range(8, 14)})
    local = jnp.where(lax.axis_index("core") == 0, local, shuffled(local, other, count))
    near = {0: 0, 1: 1, 2: 14, 3: 15, 4: 12, 5: 13, 6: 10, 7: 11, 8: 3, 9: 2, 10: 5, 11: 4, 12: 7, 13: 6, 14: 8, 15: 9}
    local = pltpu.roll(shuffled(local, near, count), lax.axis_index("z") * (NC * count), 1)
    parts = [local[:, start : start + 128] for start in range(0, width, 128)]
    folded = functools.reduce(lambda total, part: total + part, parts)
    for index, part in enumerate(parts):
        out_ref[index : index + 1, :] = part[0:1]
        out_ref[8 + index : 9 + index, :] = part[1:2]
    out_ref[7:8, :] = folded[2:3]
    halves = folded + pltpu.roll(folded, 64, 1)
    left = lax.broadcasted_iota(jnp.int32, (1, 128), 1) < 64
    out_ref[15:16, :] = jnp.where(left, halves[3:4], halves[4:5])


def gram(spread, columns, norms, line):
    vmem = pl.BlockSpec(memory_space=pltpu.VMEM)
    rows = columns.shape[1]
    width = sum(part.shape[1] for part in line)
    return pl.pallas_call(
        gram_body,
        out_shape=jax.ShapeDtypeStruct((16, 128), jnp.float32),
        in_specs=[pl.BlockSpec(memory_space=pltpu.SMEM)] + [vmem] * (2 + len(line)),
        out_specs=vmem,
        scratch_shapes=[pltpu.VMEM((2, width, D), jnp.bfloat16)],
        compiler_params=pltpu.CompilerParams(vmem_limit_bytes=20 << 20),
        cost_estimate=pl.CostEstimate(
            flops=4 * rows * width * D, bytes_accessed=4 * (rows + width) * D, transcendentals=2 * rows * width
        ),
        name="gram",
    )(spread, columns, norms, *line)


def swap(array):
    return move(array, lambda x, y, z, core: (x, y, z, 1 - core))


def around(array):
    return move(array, lambda x, y, z, core: (x, y, z + 1 - 2 * core, core))


def line_sum(array):
    other = swap(array)
    beside = [move(array, lambda x, y, z, core: (x, y, z ^ 1, core ^ flip)) for flip in range(2)]
    array = (array + other) + (beside[0] + beside[1])
    parts = [move(array, lambda x, y, z, core: (x, y, z + step, core)) for step in (2, -2, 4)]
    return ring_sum(array, parts)


def ring_parts(array, axis):
    return [
        move(array, lambda x, y, z, core: (x + step, y, z, core) if axis == "x" else (x, y + step, z, core))
        for step in (1, -1, 2)
    ]


def ring_sum(array, parts):
    return (array + parts[2]) + (parts[0] + parts[1])


def finish_body(total, count, part_ref, sums_ref, *refs):
    parts, (profiles_ref, alignment_ref) = refs[:3], refs[3:]
    far, ahead, behind = (part[...] for part in parts)
    lanes = ring_sum(sums_ref[...], [ahead, behind, far])
    sums = jnp.sum(lanes, axis=1, keepdims=True)
    sum_one, sum_two, f_cross, _, c_cross, c_one, c_two = (sums[at : at + 1, :] for at in range(7))
    left = lax.broadcasted_iota(jnp.int32, (1, 128), 1) < 64
    f_one = jnp.sum(jnp.where(left, lanes[3:4], 0.0), axis=1, keepdims=True)
    f_two = jnp.sum(jnp.where(left, 0.0, lanes[3:4]), axis=1, keepdims=True)
    h_cross = f_cross - 2.0 * c_cross / total + sum_one * sum_two / (total * total)
    h_one = f_one - 2.0 * c_one / total + sum_one * sum_one / (total * total)
    h_two = f_two - 2.0 * c_two / total + sum_two * sum_two / (total * total)
    alignment_ref[...] = h_cross / jnp.sqrt(h_one * h_two)
    width = NZ * NC * count
    first = (lax.axis_index("z") * NC + lax.axis_index("core")) * count
    for layer, c_sum in enumerate((c_one, c_two)):
        rows = jnp.concatenate([part_ref[8 * layer + at : 8 * layer + at + 1, :] for at in range(7)], axis=1)
        rows = pltpu.roll(jnp.broadcast_to(rows, (8, width)), lax.rem(width - first, width), 1)
        profiles_ref[layer : layer + 1, :] = rows[:1, :count] / jnp.sqrt(c_sum / total)


def finish(part, sums, parts, total, count):
    vmem = pl.BlockSpec(memory_space=pltpu.VMEM)
    return pl.pallas_call(
        functools.partial(finish_body, float(total), count),
        out_shape=(jax.ShapeDtypeStruct((2, count), jnp.float32), jax.ShapeDtypeStruct((1, 1), jnp.float32)),
        in_specs=[vmem] * 5,
        out_specs=(vmem, vmem),
        compiler_params=pltpu.CompilerParams(vmem_limit_bytes=2 << 20),
        name="finish",
    )(part, sums, *parts)


def shards(layer_one, layer_two, spread):
    own = lax.optimization_barrier(jnp.stack([layer_one, layer_two]))
    count = own.shape[1]
    near = [shift(own, step, 0) for step in (1, -1, 2)]
    chip = jnp.concatenate([own, swap(own)], axis=1)
    strip = jnp.concatenate([own] + near, axis=1)
    first, strip = lax.optimization_barrier((around(chip), strip))
    pieces = [strip] + [shift(strip, 0, step) for step in (1, -1, 2)]
    ring = [first]
    for _ in range(2):
        ring.append(around(ring[-1]))
    last = around(ring[2][:, :count])
    ends = jnp.concatenate([last, swap(last)], axis=1)
    line = [chip] + ring + [swap(block) for block in ring] + [ends]
    part = line_sum(gram(spread, *plane_rows(spread, pieces), line))
    r_one, r_two = part[0:7], part[8:15]
    terms = [r_one, r_two, part[7:8], part[15:16], r_one * r_two, r_one * r_one, r_two * r_two]
    sums = jnp.stack([jnp.sum(term, axis=0) for term in terms] + [jnp.zeros((128,), jnp.float32)])
    sums = ring_sum(sums, ring_parts(sums, "x"))
    ahead, behind, far = ring_parts(sums, "y")
    profiles, alignment = finish(part, sums, (far, ahead, behind), count * lax.axis_size(AXES), count)
    return (profiles, alignment.reshape(()))


def solution(mesh):
    finer = Mesh(mesh.devices.reshape(2, NZ, NY, NC, 2), AXES)
    return jax.shard_map(
        shards,
        mesh=finer,
        in_specs=(P(AXES, None), P(AXES, None), P()),
        out_specs=(P(None, AXES), P()),
        check_vma=False,
    )
```

```python
import functools
import math

import jax
import jax.numpy as jnp
from jax import lax
from jax.experimental import pallas as pl
from jax.experimental.pallas import tpu as pltpu
from jax.sharding import Mesh
from jax.sharding import PartitionSpec as P

D = 1024
AXES = ("x_hi", "z", "y", "core", "x_lo")
NX, NY, NZ, NC = (4, 4, 8, 2)
LOG2E = math.log2(math.e)


def linear(x, y, z, core):
    return (((x // 2 * NZ + z) * NY + y) * NC + core) * 2 + x % 2


def move(array, where):
    pairs = []
    for x in range(NX):
        for y in range(NY):
            for z in range(NZ):
                for core in range(NC):
                    tx, ty, tz, tcore = where(x, y, z, core)
                    pairs.append((linear(x, y, z, core), linear(tx % NX, ty % NY, tz % NZ, tcore % NC)))
    return lax.ppermute(array, AXES, pairs)


def shift(array, first, second):
    def where(x, y, z, core):
        dx, dy = (first, second) if core == 0 else (second, first)
        return x + dx, y + dy, z, core

    return move(array, where)


def fold_squares(rows):
    wide = rows.astype(jnp.float32)
    square = wide * wide
    folded = square[:, :128]
    for lane in range(128, D, 128):
        folded = folded + square[:, lane : lane + 128]
    return folded


def shuffled(array, moves, unit):
    lanes = lax.broadcasted_iota(jnp.int32, array.shape, 1)
    width = array.shape[1]
    result = array
    by_step = {}
    for old, fresh in moves.items():
        by_step.setdefault(fresh - old, []).append(fresh)
    for step, places in by_step.items():
        if step == 0:
            continue
        rolled = pltpu.roll(array, (step * unit) % width, 1)
        for place in places:
            inside = (lanes >= place * unit) & (lanes < (place + 1) * unit)
            result = jnp.where(inside, rolled, result)
    return result


def plane_body(spread_ref, *refs):
    pieces, (w_ref, norm_ref) = refs[:-2], refs[-2:]
    tall = pieces[0].shape[1]
    for layer in range(2):
        factor = LOG2E / jnp.full((1, 128), spread_ref[layer].astype(jnp.float32), jnp.float32)
        for index, piece in enumerate(pieces):
            rows = slice(index * tall, (index + 1) * tall)
            block = piece[layer]
            w_ref[layer, rows, :] = block
            norms = jnp.sum(fold_squares(block), axis=1, keepdims=True)
            norm_ref[layer, rows, :] = jnp.broadcast_to(norms, (tall, 128)) * (0.5 * factor)


def plane_rows(spread, pieces):
    vmem = pl.BlockSpec(memory_space=pltpu.VMEM)
    rows = sum(piece.shape[1] for piece in pieces)
    return pl.pallas_call(
        plane_body,
        out_shape=(
            jax.ShapeDtypeStruct((2, rows, D), jnp.bfloat16),
            jax.ShapeDtypeStruct((2, rows, 128), jnp.float32),
        ),
        in_specs=[pl.BlockSpec(memory_space=pltpu.SMEM)] + [vmem] * len(pieces),
        out_specs=(vmem, vmem),
        compiler_params=pltpu.CompilerParams(vmem_limit_bytes=16 << 20),
        cost_estimate=pl.CostEstimate(flops=4 * rows * D, bytes_accessed=8 * rows * D, transcendentals=0),
        name="plane_rows",
    )(spread, *pieces)


def gram_body(spread_ref, w_ref, norm_ref, *refs):
    line, (out_ref, z_ref) = refs[:-2], refs[-2:]
    width = z_ref.shape[1]
    scales = [jnp.full((1, 128), spread_ref[layer].astype(jnp.float32), jnp.float32) for layer in range(2)]
    factors = [LOG2E / scale for scale in scales]
    offsets = [jnp.exp(-D / scale) for scale in scales]
    at = 0
    for ref in line:
        z_ref[:, at : at + ref.shape[1], :] = ref[...]
        at += ref.shape[1]
    columns = []
    height = w_ref.shape[1] // 2
    for start in range(0, width, 256):
        spans = range(start, min(start + 256, width), 128)
        wide = lambda row: jnp.concatenate([row] * len(spans), axis=1)
        z_norms = []
        for layer in range(2):
            norms = [
                jnp.sum(fold_squares(z_ref[layer, span : span + 128, :]).T, axis=0, keepdims=True) for span in spans
            ]
            z_norms.append(jnp.concatenate(norms, axis=1) * (0.5 * wide(factors[layer])))
        lanes = 128 * len(spans)
        sums = [jnp.zeros((8, lanes), jnp.float32) for _ in range(5)]
        for top in range(0, w_ref.shape[1], height):
            kernels = []
            for layer in range(2):
                inner = lax.dot_general(
                    w_ref[layer, top : top + height, :],
                    z_ref[layer, start : start + lanes, :],
                    (((1,), (1,)), ((), ())),
                    preferred_element_type=jnp.float32,
                )
                power = inner * wide(factors[layer]) - wide(norm_ref[layer, top : top + height, :]) - z_norms[layer]
                kernels.append(jnp.exp2(power) - wide(offsets[layer]))
            one, two = kernels
            for row, term in enumerate((one, two, one * two, one * one, two * two)):
                sums[row] = sums[row] + jnp.sum(term.reshape(height // 8, 8, lanes), axis=0)
        rows = [jnp.sum(term, axis=0, keepdims=True) for term in sums]
        columns.append(jnp.concatenate(rows + [jnp.zeros((3, lanes), jnp.float32)], axis=0))
    local = jnp.concatenate(columns, axis=1)
    count = width // (NZ * NC)
    other = {0: 1, 1: 0, 14: 15, 15: 14}
    other.update({place: place + 6 for place in range(2, 8)})
    other.update({place: place - 6 for place in range(8, 14)})
    local = jnp.where(lax.axis_index("core") == 0, local, shuffled(local, other, count))
    near = {0: 0, 1: 1, 2: 14, 3: 15, 4: 12, 5: 13, 6: 10, 7: 11, 8: 3, 9: 2, 10: 5, 11: 4, 12: 7, 13: 6, 14: 8, 15: 9}
    local = pltpu.roll(shuffled(local, near, count), lax.axis_index("z") * (NC * count), 1)
    parts = [local[:, start : start + 128] for start in range(0, width, 128)]
    folded = functools.reduce(lambda total, part: total + part, parts)
    for index, part in enumerate(parts):
        out_ref[index : index + 1, :] = part[0:1]
        out_ref[8 + index : 9 + index, :] = part[1:2]
    out_ref[7:8, :] = folded[2:3]
    halves = folded + pltpu.roll(folded, 64, 1)
    left = lax.broadcasted_iota(jnp.int32, (1, 128), 1) < 64
    out_ref[15:16, :] = jnp.where(left, halves[3:4], halves[4:5])


def gram(spread, columns, norms, line):
    vmem = pl.BlockSpec(memory_space=pltpu.VMEM)
    rows = columns.shape[1]
    width = sum(part.shape[1] for part in line)
    return pl.pallas_call(
        gram_body,
        out_shape=jax.ShapeDtypeStruct((16, 128), jnp.float32),
        in_specs=[pl.BlockSpec(memory_space=pltpu.SMEM)] + [vmem] * (2 + len(line)),
        out_specs=vmem,
        scratch_shapes=[pltpu.VMEM((2, width, D), jnp.bfloat16)],
        compiler_params=pltpu.CompilerParams(vmem_limit_bytes=20 << 20),
        cost_estimate=pl.CostEstimate(
            flops=4 * rows * width * D, bytes_accessed=4 * (rows + width) * D, transcendentals=2 * rows * width
        ),
        name="gram",
    )(spread, columns, norms, *line)


def swap(array):
    return move(array, lambda x, y, z, core: (x, y, z, 1 - core))


def around(array):
    return move(array, lambda x, y, z, core: (x, y, z + 1 - 2 * core, core))


def line_sum(array):
    other = swap(array)
    beside = [move(array, lambda x, y, z, core: (x, y, z ^ 1, core ^ flip)) for flip in range(2)]
    array = (array + other) + (beside[0] + beside[1])
    parts = [move(array, lambda x, y, z, core: (x, y, z + step, core)) for step in (2, -2, 4)]
    return ring_sum(array, parts)


def ring_parts(array, axis):
    return [
        move(array, lambda x, y, z, core: (x + step, y, z, core) if axis == "x" else (x, y + step, z, core))
        for step in (1, -1, 2)
    ]


def ring_sum(array, parts):
    return (array + parts[2]) + (parts[0] + parts[1])


def finish_body(total, count, part_ref, sums_ref, *refs):
    parts, (profiles_ref, alignment_ref) = refs[:3], refs[3:]
    far, ahead, behind = (part[...] for part in parts)
    lanes = ring_sum(sums_ref[...], [ahead, behind, far])
    sums = jnp.sum(lanes, axis=1, keepdims=True)
    sum_one, sum_two, f_cross, _, c_cross, c_one, c_two = (sums[at : at + 1, :] for at in range(7))
    left = lax.broadcasted_iota(jnp.int32, (1, 128), 1) < 64
    f_one = jnp.sum(jnp.where(left, lanes[3:4], 0.0), axis=1, keepdims=True)
    f_two = jnp.sum(jnp.where(left, 0.0, lanes[3:4]), axis=1, keepdims=True)
    h_cross = f_cross - 2.0 * c_cross / total + sum_one * sum_two / (total * total)
    h_one = f_one - 2.0 * c_one / total + sum_one * sum_one / (total * total)
    h_two = f_two - 2.0 * c_two / total + sum_two * sum_two / (total * total)
    alignment_ref[...] = h_cross / jnp.sqrt(h_one * h_two)
    width = NZ * NC * count
    first = (lax.axis_index("z") * NC + lax.axis_index("core")) * count
    for layer, c_sum in enumerate((c_one, c_two)):
        rows = jnp.concatenate([part_ref[8 * layer + at : 8 * layer + at + 1, :] for at in range(7)], axis=1)
        rows = pltpu.roll(jnp.broadcast_to(rows, (8, width)), lax.rem(width - first, width), 1)
        profiles_ref[layer : layer + 1, :] = rows[:1, :count] / jnp.sqrt(c_sum / total)


def finish(part, sums, parts, total, count):
    vmem = pl.BlockSpec(memory_space=pltpu.VMEM)
    return pl.pallas_call(
        functools.partial(finish_body, float(total), count),
        out_shape=(jax.ShapeDtypeStruct((2, count), jnp.float32), jax.ShapeDtypeStruct((1, 1), jnp.float32)),
        in_specs=[vmem] * 5,
        out_specs=(vmem, vmem),
        compiler_params=pltpu.CompilerParams(vmem_limit_bytes=2 << 20),
        name="finish",
    )(part, sums, *parts)


def shards(layer_one, layer_two, spread):
    own = lax.optimization_barrier(jnp.stack([layer_one, layer_two]))
    count = own.shape[1]
    near = [shift(own, step, 0) for step in (1, -1, 2)]
    far = move(own, lambda x, y, z, core: (x, y, z + 4, core))
    chip = jnp.concatenate([own, swap(own)], axis=1)
    strip = jnp.concatenate([own] + near, axis=1)
    chip, strip, far = lax.optimization_barrier((chip, strip, far))
    pieces = [strip] + [shift(strip, 0, step) for step in (1, -1, 2)]
    ring = [around(chip)]
    for _ in range(2):
        ring.append(around(ring[-1]))
    ends = jnp.concatenate([far, swap(far)], axis=1)
    pieces, late = lax.optimization_barrier((pieces, ring[2]))
    line = [chip] + ring + [swap(ring[0]), swap(ring[1]), swap(late)] + [ends]
    part = line_sum(gram(spread, *plane_rows(spread, pieces), line))
    r_one, r_two = part[0:7], part[8:15]
    terms = [r_one, r_two, part[7:8], part[15:16], r_one * r_two, r_one * r_one, r_two * r_two]
    sums = jnp.stack([jnp.sum(term, axis=0) for term in terms] + [jnp.zeros((128,), jnp.float32)])
    sums = ring_sum(sums, ring_parts(sums, "x"))
    ahead, behind, far = ring_parts(sums, "y")
    profiles, alignment = finish(part, sums, (far, ahead, behind), count * lax.axis_size(AXES), count)
    return (profiles, alignment.reshape(()))


def solution(mesh):
    finer = Mesh(mesh.devices.reshape(2, NZ, NY, NC, 2), AXES)
    return jax.shard_map(
        shards,
        mesh=finer,
        in_specs=(P(AXES, None), P(AXES, None), P()),
        out_specs=(P(None, AXES), P()),
        check_vma=False,
    )
```

```python
import functools
import math

import jax
import jax.numpy as jnp
from jax import lax
from jax.experimental import pallas as pl
from jax.experimental.pallas import tpu as pltpu
from jax.sharding import Mesh
from jax.sharding import PartitionSpec as P

D = 1024
AXES = ("x_hi", "z", "y", "core", "x_lo")
NX, NY, NZ, NC = (4, 4, 8, 2)
LOG2E = math.log2(math.e)


def linear(x, y, z, core):
    return (((x // 2 * NZ + z) * NY + y) * NC + core) * 2 + x % 2


def move(array, where):
    pairs = []
    for x in range(NX):
        for y in range(NY):
            for z in range(NZ):
                for core in range(NC):
                    tx, ty, tz, tcore = where(x, y, z, core)
                    pairs.append((linear(x, y, z, core), linear(tx % NX, ty % NY, tz % NZ, tcore % NC)))
    return lax.ppermute(array, AXES, pairs)


def shift(array, first, second):
    def where(x, y, z, core):
        dx, dy = (first, second) if core == 0 else (second, first)
        return x + dx, y + dy, z, core

    return move(array, where)


def fold_squares(rows):
    wide = rows.astype(jnp.float32)
    square = wide * wide
    folded = square[:, :128]
    for lane in range(128, D, 128):
        folded = folded + square[:, lane : lane + 128]
    return folded


def shuffled(array, moves, unit):
    lanes = lax.broadcasted_iota(jnp.int32, array.shape, 1)
    width = array.shape[1]
    result = array
    by_step = {}
    for old, fresh in moves.items():
        by_step.setdefault(fresh - old, []).append(fresh)
    for step, places in by_step.items():
        if step == 0:
            continue
        rolled = pltpu.roll(array, (step * unit) % width, 1)
        for place in places:
            inside = (lanes >= place * unit) & (lanes < (place + 1) * unit)
            result = jnp.where(inside, rolled, result)
    return result


def plane_body(spread_ref, *refs):
    pieces, (w_ref, norm_ref) = refs[:-2], refs[-2:]
    tall = pieces[0].shape[1]
    for layer in range(2):
        factor = LOG2E / jnp.full((1, 128), spread_ref[layer].astype(jnp.float32), jnp.float32)
        for index, piece in enumerate(pieces):
            rows = slice(index * tall, (index + 1) * tall)
            block = piece[layer]
            w_ref[layer, rows, :] = block
            norms = jnp.sum(fold_squares(block), axis=1, keepdims=True)
            norm_ref[layer, rows, :] = jnp.broadcast_to(norms, (tall, 128)) * (0.5 * factor)


def plane_rows(spread, pieces):
    vmem = pl.BlockSpec(memory_space=pltpu.VMEM)
    rows = sum(piece.shape[1] for piece in pieces)
    return pl.pallas_call(
        plane_body,
        out_shape=(
            jax.ShapeDtypeStruct((2, rows, D), jnp.bfloat16),
            jax.ShapeDtypeStruct((2, rows, 128), jnp.float32),
        ),
        in_specs=[pl.BlockSpec(memory_space=pltpu.SMEM)] + [vmem] * len(pieces),
        out_specs=(vmem, vmem),
        compiler_params=pltpu.CompilerParams(vmem_limit_bytes=16 << 20),
        cost_estimate=pl.CostEstimate(flops=4 * rows * D, bytes_accessed=8 * rows * D, transcendentals=0),
        name="plane_rows",
    )(spread, *pieces)


def gram_body(spread_ref, w_ref, norm_ref, *refs):
    line, (out_ref, z_ref) = refs[:-2], refs[-2:]
    width = z_ref.shape[1]
    scales = [jnp.full((1, 128), spread_ref[layer].astype(jnp.float32), jnp.float32) for layer in range(2)]
    factors = [LOG2E / scale for scale in scales]
    offsets = [jnp.exp(-D / scale) for scale in scales]
    at = 0
    for ref in line:
        z_ref[:, at : at + ref.shape[1], :] = ref[...]
        at += ref.shape[1]
    columns = []
    height = w_ref.shape[1] // 2
    for start in range(0, width, 256):
        spans = range(start, min(start + 256, width), 128)
        wide = lambda row: jnp.concatenate([row] * len(spans), axis=1)
        z_norms = []
        for layer in range(2):
            norms = [
                jnp.sum(fold_squares(z_ref[layer, span : span + 128, :]).T, axis=0, keepdims=True) for span in spans
            ]
            z_norms.append(jnp.concatenate(norms, axis=1) * (0.5 * wide(factors[layer])))
        lanes = 128 * len(spans)
        sums = [jnp.zeros((8, lanes), jnp.float32) for _ in range(5)]
        for top in range(0, w_ref.shape[1], height):
            kernels = []
            for layer in range(2):
                inner = lax.dot_general(
                    w_ref[layer, top : top + height, :],
                    z_ref[layer, start : start + lanes, :],
                    (((1,), (1,)), ((), ())),
                    preferred_element_type=jnp.float32,
                )
                power = inner * wide(factors[layer]) - wide(norm_ref[layer, top : top + height, :]) - z_norms[layer]
                kernels.append(jnp.exp2(power) - wide(offsets[layer]))
            one, two = kernels
            for row, term in enumerate((one, two, one * two, one * one, two * two)):
                sums[row] = sums[row] + jnp.sum(term.reshape(height // 8, 8, lanes), axis=0)
        rows = [jnp.sum(term, axis=0, keepdims=True) for term in sums]
        columns.append(jnp.concatenate(rows + [jnp.zeros((3, lanes), jnp.float32)], axis=0))
    local = jnp.concatenate(columns, axis=1)
    count = width // (NZ * NC)
    other = {0: 1, 1: 0, 14: 15, 15: 14}
    other.update({place: place + 6 for place in range(2, 8)})
    other.update({place: place - 6 for place in range(8, 14)})
    local = jnp.where(lax.axis_index("core") == 0, local, shuffled(local, other, count))
    near = {0: 0, 1: 1, 2: 14, 3: 15, 4: 12, 5: 13, 6: 10, 7: 11, 8: 3, 9: 2, 10: 5, 11: 4, 12: 7, 13: 6, 14: 8, 15: 9}
    local = pltpu.roll(shuffled(local, near, count), lax.axis_index("z") * (NC * count), 1)
    parts = [local[:, start : start + 128] for start in range(0, width, 128)]
    folded = functools.reduce(lambda total, part: total + part, parts)
    for index, part in enumerate(parts):
        out_ref[index : index + 1, :] = part[0:1]
        out_ref[8 + index : 9 + index, :] = part[1:2]
    out_ref[7:8, :] = folded[2:3]
    halves = folded + pltpu.roll(folded, 64, 1)
    left = lax.broadcasted_iota(jnp.int32, (1, 128), 1) < 64
    out_ref[15:16, :] = jnp.where(left, halves[3:4], halves[4:5])


def gram(spread, columns, norms, line):
    vmem = pl.BlockSpec(memory_space=pltpu.VMEM)
    rows = columns.shape[1]
    width = sum(part.shape[1] for part in line)
    return pl.pallas_call(
        gram_body,
        out_shape=jax.ShapeDtypeStruct((16, 128), jnp.float32),
        in_specs=[pl.BlockSpec(memory_space=pltpu.SMEM)] + [vmem] * (2 + len(line)),
        out_specs=vmem,
        scratch_shapes=[pltpu.VMEM((2, width, D), jnp.bfloat16)],
        compiler_params=pltpu.CompilerParams(vmem_limit_bytes=20 << 20),
        cost_estimate=pl.CostEstimate(
            flops=4 * rows * width * D, bytes_accessed=4 * (rows + width) * D, transcendentals=2 * rows * width
        ),
        name="gram",
    )(spread, columns, norms, *line)


def swap(array):
    return move(array, lambda x, y, z, core: (x, y, z, 1 - core))


def around(array):
    return move(array, lambda x, y, z, core: (x, y, z + 1 - 2 * core, core))


def line_sum(array):
    other = swap(array)
    beside = [move(array, lambda x, y, z, core: (x, y, z ^ 1, core ^ flip)) for flip in range(2)]
    array = (array + other) + (beside[0] + beside[1])
    parts = [move(array, lambda x, y, z, core: (x, y, z + step, core)) for step in (2, -2, 4)]
    return ring_sum(array, parts)


def ring_parts(array, axis):
    return [
        move(array, lambda x, y, z, core: (x + step, y, z, core) if axis == "x" else (x, y + step, z, core))
        for step in (1, -1, 2)
    ]


def ring_sum(array, parts):
    return (array + parts[2]) + (parts[0] + parts[1])


def finish_body(total, count, part_ref, sums_ref, *refs):
    parts, (profiles_ref, alignment_ref) = refs[:3], refs[3:]
    far, ahead, behind = (part[...] for part in parts)
    lanes = ring_sum(sums_ref[...], [ahead, behind, far])
    sums = jnp.sum(lanes, axis=1, keepdims=True)
    sum_one, sum_two, f_cross, _, c_cross, c_one, c_two = (sums[at : at + 1, :] for at in range(7))
    left = lax.broadcasted_iota(jnp.int32, (1, 128), 1) < 64
    f_one = jnp.sum(jnp.where(left, lanes[3:4], 0.0), axis=1, keepdims=True)
    f_two = jnp.sum(jnp.where(left, 0.0, lanes[3:4]), axis=1, keepdims=True)
    h_cross = f_cross - 2.0 * c_cross / total + sum_one * sum_two / (total * total)
    h_one = f_one - 2.0 * c_one / total + sum_one * sum_one / (total * total)
    h_two = f_two - 2.0 * c_two / total + sum_two * sum_two / (total * total)
    alignment_ref[...] = h_cross / jnp.sqrt(h_one * h_two)
    width = NZ * NC * count
    first = (lax.axis_index("z") * NC + lax.axis_index("core")) * count
    for layer, c_sum in enumerate((c_one, c_two)):
        rows = jnp.concatenate([part_ref[8 * layer + at : 8 * layer + at + 1, :] for at in range(7)], axis=1)
        rows = pltpu.roll(jnp.broadcast_to(rows, (8, width)), lax.rem(width - first, width), 1)
        profiles_ref[layer : layer + 1, :] = rows[:1, :count] / jnp.sqrt(c_sum / total)


def finish(part, sums, parts, total, count):
    vmem = pl.BlockSpec(memory_space=pltpu.VMEM)
    return pl.pallas_call(
        functools.partial(finish_body, float(total), count),
        out_shape=(jax.ShapeDtypeStruct((2, count), jnp.float32), jax.ShapeDtypeStruct((1, 1), jnp.float32)),
        in_specs=[vmem] * 5,
        out_specs=(vmem, vmem),
        compiler_params=pltpu.CompilerParams(vmem_limit_bytes=2 << 20),
        name="finish",
    )(part, sums, *parts)


def shards(layer_one, layer_two, spread):
    own = lax.optimization_barrier(jnp.stack([layer_one, layer_two]))
    count = own.shape[1]
    near = [shift(own, step, 0) for step in (1, -1, 2)]
    chip = jnp.concatenate([own, swap(own)], axis=1)
    strip = jnp.concatenate([own] + near, axis=1)
    first, strip = lax.optimization_barrier((around(chip), strip))
    pieces = [strip] + [shift(strip, 0, step) for step in (1, -1, 2)]
    ring = [first]
    for _ in range(2):
        ring.append(around(ring[-1]))
    last = around(ring[2][:, :count])
    ends = jnp.concatenate([last, swap(last)], axis=1)
    early = swap(jnp.concatenate(ring[:2], axis=1))
    line = [chip] + ring + [early, swap(ring[2]), ends]
    part = line_sum(gram(spread, *plane_rows(spread, pieces), line))
    r_one, r_two = part[0:7], part[8:15]
    terms = [r_one, r_two, part[7:8], part[15:16], r_one * r_two, r_one * r_one, r_two * r_two]
    sums = jnp.stack([jnp.sum(term, axis=0) for term in terms] + [jnp.zeros((128,), jnp.float32)])
    sums = ring_sum(sums, ring_parts(sums, "x"))
    ahead, behind, far = ring_parts(sums, "y")
    profiles, alignment = finish(part, sums, (far, ahead, behind), count * lax.axis_size(AXES), count)
    return (profiles, alignment.reshape(()))


def solution(mesh):
    finer = Mesh(mesh.devices.reshape(2, NZ, NY, NC, 2), AXES)
    return jax.shard_map(
        shards,
        mesh=finer,
        in_specs=(P(AXES, None), P(AXES, None), P()),
        out_specs=(P(None, AXES), P()),
        check_vma=False,
    )
```
